32 devices in a mesh: row: 2 (over x), col: 16 (over z, y, core).
Axes of the slice: x: 2, y: 2, z: 4, core: 2. Of those that a mesh axis runs over, the one named last changes fastest.
Arguments:
- hessian_old: float32 [2048, 12288], P('row', 'col'), may hold values from -6 to 6
- gate_rows: bfloat16 [512, 2048], P('col', 'row'), may hold values from -9 to 9
- up_rows: bfloat16 [512, 2048], P('col', 'row'), may hold values from -15 to 15
- gate_columns: bfloat16 [512, 12288], P('row', 'col'), may hold values from -9 to 9
- up_columns: bfloat16 [512, 12288], P('row', 'col'), may hold values from -15 to 15
Outputs:
- hessian_new: float32 [2048, 12288], P('row', 'col')
The draws below stay inside these ranges and needn't reach their ends.
All inputs are finite; a program needn't handle non-finite values.
Results may differ from the reference program's by a relative error of at most 0.00099.
Values may be sent and summed in bfloat16 or wider, within the bound.
A program may use at most 64 MiB of HBM per device.

```python
import jax
import jax.numpy as jnp
from jax import lax

TOKENS = 512
ROWS = 2048
COLS = 12288


def block_scale(key, shape, split, low, high):
    def one(axis_at, shards_of):
        heights = jax.random.uniform(jax.random.fold_in(jax.random.fold_in(key, 6), axis_at), (shards_of,), jnp.float32, low / len(split), high / len(split))
        return jnp.repeat(jnp.exp(heights), shape[axis_at] // shards_of).reshape((-1,) + (1,) * (len(shape) - axis_at - 1))

    level = one(*split[0])
    for cut in split[1:]:
        level = level * one(*cut)
    return level


def gaussian(key, shape, spread, bound, split=(), held_as=jnp.bfloat16):
    loudness = block_scale(key, shape, split, -0.22, 0.18) if split else 1.0
    array = jax.random.normal(key, shape, jnp.float32) * spread * loudness
    return jnp.minimum(jnp.maximum(array, -bound), bound).astype(held_as)


def setup_inputs(seed: int = 0) -> dict:
    splits = jax.random.split(jax.random.key(seed), 6)
    hessian_old = gaussian(splits[0], (ROWS, COLS), 1.0, 6.0, ((0, 2), (1, 16)), jnp.float32)
    gate_rows = gaussian(splits[1], (TOKENS, ROWS), 1.5, 9.0, ((0, 16), (1, 2)))
    up_rows = gaussian(splits[2], (TOKENS, ROWS), 2.5, 15.0, ((0, 16), (1, 2)))
    gate_columns = gaussian(splits[3], (TOKENS, COLS), 1.5, 9.0, ((0, 2), (1, 16)))
    up_columns = gaussian(splits[4], (TOKENS, COLS), 2.5, 15.0, ((0, 2), (1, 16)))
    return dict(hessian_old=hessian_old, gate_rows=gate_rows, up_rows=up_rows, gate_columns=gate_columns, up_columns=up_columns)


def silu_product(gate, up):
    return (jax.nn.silu(gate.astype(jnp.float32)) * up.astype(jnp.float32)).astype(jnp.bfloat16)


def reference(hessian_old, gate_rows, up_rows, gate_columns, up_columns):
    row_inputs = silu_product(gate_rows, up_rows)
    column_inputs = silu_product(gate_columns, up_columns)
    product = lax.dot_general(row_inputs, column_inputs, (((0,), (0,)), ((), ())), preferred_element_type=jnp.float32)
    return 0.5 * hessian_old + product / TOKENS
```

```python
import functools

import jax
import jax.numpy as jnp
from jax import lax
from jax.experimental import pallas as pl
from jax.experimental.pallas import tpu as pltpu
from jax.sharding import PartitionSpec as P

MESH = pl.DeviceIdType.MESH


def silu_product(gate, up):
    return (jax.nn.silu(gate.astype(jnp.float32)) * up.astype(jnp.float32)).astype(jnp.bfloat16)


def partner(z, d, size):
    if size & (size - 1):
        return lax.rem(z + d, size), lax.rem(z + size - d, size)
    out, bit = z, 1
    while bit < size:
        if d & bit:
            out = out + bit * (1 - 2 * lax.rem(z // bit, 2))
        bit *= 2
    return out, out


def kernel(dims, old_hbm, gr_hbm, ur_hbm, gc_hbm, uc_hbm, out_ref, old, gr, ur, gc, uc, rows, cols, in_sem, old_sem, z_sem, y_sem, k_sem, x_sem, row_recv, col_recv):
    n_row, n_z, n_y, n_k, tiles, width, block = dims
    n_col = n_z * n_y * n_k
    depth = gc.shape[1]
    height = out_ref.shape[0]
    tokens = n_col * gr.shape[0]
    r = lax.axis_index("row")
    c = lax.axis_index("col")
    k = lax.rem(c, n_k)
    y = lax.rem(c // n_k, n_y)
    z = c // (n_k * n_y)

    def at(z_, y_, k_):
        return (z_ * n_y + y_) * n_k + k_

    z_to = [partner(z, d, n_z)[0] for d in range(n_z - 1, 0, -1)]
    z_from = [partner(z, d, n_z)[1] for d in range(n_z - 1, 0, -1)]
    other_y = [lax.rem(y + 1, n_y)] if n_y > 1 else []
    other_k = [lax.rem(k + 1, n_k)] if n_k > 1 else []
    r_to = [lax.rem(r + d, n_row) for d in range(1, n_row)]
    r_from = [lax.rem(r + n_row - d, n_row) for d in range(1, n_row)]

    barrier = pltpu.get_barrier_semaphore()
    peers = [{"col": at(t, y, k)} for t in z_to] + [{"col": at(z, t, k)} for t in other_y] + [{"col": at(z, y, t)} for t in other_k]
    peers += [{"row": t} for t in r_to]
    for peer in peers:
        pl.semaphore_signal(barrier, inc=1, device_id=peer, device_id_type=MESH)

    loads = [pltpu.make_async_copy(gr_hbm, gr, in_sem.at[0]), pltpu.make_async_copy(ur_hbm, ur, in_sem.at[1])]
    for j in range(tiles):
        part = pl.ds(j * width, width)
        loads.append(pltpu.make_async_copy(gc_hbm.at[:, part], gc.at[j], in_sem.at[2 + 2 * j]))
        loads.append(pltpu.make_async_copy(uc_hbm.at[:, part], uc.at[j], in_sem.at[3 + 2 * j]))
    for load in loads:
        load.start()
    old_load = pltpu.make_async_copy(old_hbm, old, old_sem)
    old_load.start()

    started = []

    def send_row(piece, sem, device):
        copy = pltpu.make_async_remote_copy(
            src_ref=rows.at[piece], dst_ref=rows.at[piece], send_sem=sem, recv_sem=row_recv.at[piece],
            device_id={"col": device}, device_id_type=MESH)
        copy.start()
        started.append(copy)

    def wait_row(piece):
        pltpu.make_async_remote_copy(
            src_ref=rows.at[piece], dst_ref=rows.at[piece], send_sem=k_sem.at[0], recv_sem=row_recv.at[piece],
            device_id={"col": c}, device_id_type=MESH).wait_recv()

    loads[0].wait()
    loads[1].wait()
    rows[c] = silu_product(gr[...], ur[...])
    loads[2].wait()
    loads[3].wait()
    cols[r, 0] = silu_product(gc[0], uc[0])
    pl.semaphore_wait(barrier, len(peers))

    for i, t in enumerate(z_to):
        send_row(c, z_sem.at[i], at(t, y, k))
    for t in other_y:
        send_row(c, y_sem.at[0], at(z, t, k))
    for t in other_k:
        send_row(c, k_sem.at[0], at(z, y, t))
    for j in range(tiles):
        if j:
            loads[2 + 2 * j].wait()
            loads[3 + 2 * j].wait()
            cols[r, j] = silu_product(gc[j], uc[j])
        for i, t in enumerate(r_to):
            copy = pltpu.make_async_remote_copy(
                src_ref=cols.at[r, j], dst_ref=cols.at[r, j], send_sem=x_sem.at[i, j], recv_sem=col_recv.at[r, j],
                device_id={"row": t}, device_id_type=MESH)
            copy.start()
            started.append(copy)

    used = 1

    def pass_on(piece):
        nonlocal used
        for t in other_k:
            send_row(piece, k_sem.at[used], at(z, y, t))
        used += 1

    for t in other_y:
        wait_row(at(z, t, k))
        pass_on(at(z, t, k))
    for i, s in enumerate(z_from):
        wait_row(at(s, y, k))
        for t in other_y:
            send_row(at(s, y, k), y_sem.at[1 + i], at(z, t, k))
        pass_on(at(s, y, k))
    for s in z_from:
        for t in other_y:
            wait_row(at(s, t, k))
            pass_on(at(s, t, k))
    for t in other_k:
        wait_row(at(z, y, t))
        for u in other_y:
            wait_row(at(z, u, t))
        for s in z_from:
            wait_row(at(s, y, t))
        for s in z_from:
            for u in other_y:
                wait_row(at(s, u, t))
    for s in r_from:
        for j in range(tiles):
            pltpu.make_async_remote_copy(
                src_ref=cols.at[s, j], dst_ref=cols.at[s, j], send_sem=x_sem.at[0, 0], recv_sem=col_recv.at[s, j],
                device_id={"row": r}, device_id_type=MESH).wait_recv()
    old_load.wait()

    share = n_col // n_row

    @pl.loop(0, height // block)
    def _(m):
        here = pl.ds(pl.multiple_of(m * block, block), block)
        for j in range(tiles):
            there = pl.ds(j * width, width)
            total = None
            for s in range(n_row):
                left = rows[pl.ds(s * share, share), :, here].reshape(depth, block)
                term = lax.dot_general(left, cols[s, j], (((0,), (0,)), ((), ())), preferred_element_type=jnp.float32)
                total = term if total is None else total + term
            total = total * (1.0 / tokens) if tokens & (tokens - 1) == 0 else total / tokens
            out_ref[here, there] = 0.5 * old[here, there] + total

    for copy in started:
        copy.wait_send()


def body(n_row, n_col, hessian_old, gate_rows, up_rows, gate_columns, up_columns):
    n_k = 2 if n_col % 2 == 0 else 1
    n_y = 2 if (n_col // n_k) % 2 == 0 else 1
    n_z = n_col // (n_k * n_y)
    height, span = hessian_old.shape
    piece = gate_rows.shape[0]
    depth = gate_columns.shape[0]
    width = 256 if span % 256 == 0 else span
    block = 256 if height % 256 == 0 else height
    tiles = span // width
    hbm_spec = pl.BlockSpec(memory_space=pltpu.HBM)
    return pl.pallas_call(
        functools.partial(kernel, (n_row, n_z, n_y, n_k, tiles, width, block)),
        out_shape=jax.ShapeDtypeStruct(hessian_old.shape, jnp.float32),
        in_specs=[hbm_spec] * 5,
        out_specs=pl.BlockSpec(memory_space=pltpu.VMEM),
        scratch_shapes=[
            pltpu.VMEM((height, span), jnp.float32),
            pltpu.VMEM((piece, height), jnp.bfloat16),
            pltpu.VMEM((piece, height), jnp.bfloat16),
            pltpu.VMEM((tiles, depth, width), jnp.bfloat16),
            pltpu.VMEM((tiles, depth, width), jnp.bfloat16),
            pltpu.VMEM((n_col, piece, height), jnp.bfloat16),
            pltpu.VMEM((n_row, tiles, depth, width), jnp.bfloat16),
            pltpu.SemaphoreType.DMA((2 + 2 * tiles,)),
            pltpu.SemaphoreType.DMA,
            pltpu.SemaphoreType.DMA((max(n_z - 1, 1),)),
            pltpu.SemaphoreType.DMA((n_z,)),
            pltpu.SemaphoreType.DMA((n_z * n_y,)),
            pltpu.SemaphoreType.DMA((max(n_row - 1, 1), tiles)),
            pltpu.SemaphoreType.DMA((n_col,)),
            pltpu.SemaphoreType.DMA((n_row, tiles)),
        ],
        compiler_params=pltpu.CompilerParams(collective_id=0, has_side_effects=True, vmem_limit_bytes=40 * 1024 * 1024),
        name="update",
    )(hessian_old, gate_rows, up_rows, gate_columns, up_columns)


def solution(mesh):
    in_specs = (P("row", "col"), P("col", "row"), P("col", "row"), P("row", "col"), P("row", "col"))
    out_specs = P("row", "col")
    step = functools.partial(body, mesh.shape["row"], mesh.shape["col"])
    return jax.shard_map(step, mesh=mesh, in_specs=in_specs, out_specs=out_specs, check_vma=False)
```

```python
import functools

import jax
import jax.numpy as jnp
from jax import lax
from jax.experimental import pallas as pl
from jax.experimental.pallas import tpu as pltpu
from jax.sharding import PartitionSpec as P

MESH = pl.DeviceIdType.MESH


def silu_product(gate, up):
    return (jax.nn.silu(gate.astype(jnp.float32)) * up.astype(jnp.float32)).astype(jnp.bfloat16)


def partner(z, d, size):
    if size & (size - 1):
        return lax.rem(z + d, size), lax.rem(z + size - d, size)
    out, bit = z, 1
    while bit < size:
        if d & bit:
            out = out + bit * (1 - 2 * lax.rem(z // bit, 2))
        bit *= 2
    return out, out


def gather_kernel(dims, old_hbm, gr_hbm, ur_hbm, gc_hbm, uc_hbm, old, rows, cols, gr, ur, gc, uc, in_sem, old_sem, z_sem, y_sem, k_sem, x_sem, row_recv, col_recv):
    n_row, n_z, n_y, n_k, tiles, width = dims
    n_col = n_z * n_y * n_k
    r = lax.axis_index("row")
    c = lax.axis_index("col")
    k = lax.rem(c, n_k)
    y = lax.rem(c // n_k, n_y)
    z = c // (n_k * n_y)

    def at(z_, y_, k_):
        return (z_ * n_y + y_) * n_k + k_

    z_to = [partner(z, d, n_z)[0] for d in range(1, n_z)]
    z_from = [partner(z, d, n_z)[1] for d in range(1, n_z)]
    other_y = [lax.rem(y + 1, n_y)] if n_y > 1 else []
    other_k = [lax.rem(k + 1, n_k)] if n_k > 1 else []
    r_to = [lax.rem(r + d, n_row) for d in range(1, n_row)]
    r_from = [lax.rem(r + n_row - d, n_row) for d in range(1, n_row)]

    barrier = pltpu.get_barrier_semaphore()
    peers = [{"col": at(t, y, k)} for t in z_to] + [{"col": at(z, t, k)} for t in other_y] + [{"col": at(z, y, t)} for t in other_k]
    peers += [{"row": t} for t in r_to]
    for peer in peers:
        pl.semaphore_signal(barrier, inc=1, device_id=peer, device_id_type=MESH)

    loads = [pltpu.make_async_copy(gr_hbm, gr, in_sem.at[0]), pltpu.make_async_copy(ur_hbm, ur, in_sem.at[1])]
    for j in range(tiles):
        part = pl.ds(j * width, width)
        loads.append(pltpu.make_async_copy(gc_hbm.at[:, part], gc.at[j], in_sem.at[2 + 2 * j]))
        loads.append(pltpu.make_async_copy(uc_hbm.at[:, part], uc.at[j], in_sem.at[3 + 2 * j]))
    for load in loads:
        load.start()
    old_load = pltpu.make_async_copy(old_hbm, old, old_sem)
    old_load.start()

    started = []

    def send_row(piece, sem, device):
        copy = pltpu.make_async_remote_copy(
            src_ref=rows.at[piece], dst_ref=rows.at[piece], send_sem=sem, recv_sem=row_recv.at[piece],
            device_id={"col": device}, device_id_type=MESH)
        copy.start()
        started.append(copy)

    def wait_row(piece):
        pltpu.make_async_remote_copy(
            src_ref=rows.at[piece], dst_ref=rows.at[piece], send_sem=k_sem.at[0], recv_sem=row_recv.at[piece],
            device_id={"col": c}, device_id_type=MESH).wait_recv()

    loads[0].wait()
    loads[1].wait()
    rows[c] = silu_product(gr[...], ur[...])
    loads[2].wait()
    loads[3].wait()
    cols[r, 0] = silu_product(gc[0], uc[0])
    pl.semaphore_wait(barrier, len(peers))

    for i, t in enumerate(z_to):
        send_row(c, z_sem.at[i], at(t, y, k))
    for t in other_y:
        send_row(c, y_sem.at[0], at(z, t, k))
    for t in other_k:
        send_row(c, k_sem.at[0], at(z, y, t))
    for j in range(tiles):
        if j:
            loads[2 + 2 * j].wait()
            loads[3 + 2 * j].wait()
            cols[r, j] = silu_product(gc[j], uc[j])
        for i, t in enumerate(r_to):
            copy = pltpu.make_async_remote_copy(
                src_ref=cols.at[r, j], dst_ref=cols.at[r, j], send_sem=x_sem.at[i, j], recv_sem=col_recv.at[r, j],
                device_id={"row": t}, device_id_type=MESH)
            copy.start()
            started.append(copy)

    used = 1

    def pass_on(piece):
        nonlocal used
        for t in other_k:
            send_row(piece, k_sem.at[used], at(z, y, t))
        used += 1

    for t in other_y:
        wait_row(at(z, t, k))
        pass_on(at(z, t, k))
    for i, s in enumerate(z_from):
        wait_row(at(s, y, k))
        for t in other_y:
            send_row(at(s, y, k), y_sem.at[1 + i], at(z, t, k))
        pass_on(at(s, y, k))
    for s in z_from:
        for t in other_y:
            wait_row(at(s, t, k))
            pass_on(at(s, t, k))
    for t in other_k:
        wait_row(at(z, y, t))
        for u in other_y:
            wait_row(at(z, u, t))
        for s in z_from:
            wait_row(at(s, y, t))
        for s in z_from:
            for u in other_y:
                wait_row(at(s, u, t))
    for s in r_from:
        for j in range(tiles):
            pltpu.make_async_remote_copy(
                src_ref=cols.at[s, j], dst_ref=cols.at[s, j], send_sem=x_sem.at[0, 0], recv_sem=col_recv.at[s, j],
                device_id={"row": r}, device_id_type=MESH).wait_recv()
    old_load.wait()

    for copy in started:
        copy.wait_send()


def product_kernel(block, old, rows, cols, out_hbm, out, sem):
    n_col, piece, height = rows.shape
    n_row, tiles, depth, width = cols.shape
    tokens = n_col * piece
    share = n_col // n_row
    stores = []
    for m in range(height // block):
        here = pl.ds(m * block, block)
        for j in range(tiles):
            there = pl.ds(j * width, width)
            total = None
            for s in range(n_row):
                left = rows[pl.ds(s * share, share), :, here].reshape(depth, block)
                term = lax.dot_general(left, cols[s, j], (((0,), (0,)), ((), ())), preferred_element_type=jnp.float32)
                total = term if total is None else total + term
            total = total * (1.0 / tokens) if tokens & (tokens - 1) == 0 else total / tokens
            out[here, there] = 0.5 * old[here, there] + total
        store = pltpu.make_async_copy(out.at[here], out_hbm.at[here], sem.at[m])
        store.start()
        stores.append(store)
    for store in stores:
        store.wait()


def body(n_row, n_col, hessian_old, gate_rows, up_rows, gate_columns, up_columns):
    n_k = 2 if n_col % 2 == 0 else 1
    n_y = 2 if (n_col // n_k) % 2 == 0 else 1
    n_z = n_col // (n_k * n_y)
    height, span = hessian_old.shape
    piece = gate_rows.shape[0]
    depth = gate_columns.shape[0]
    width = 256 if span % 256 == 0 else span
    block = 128 if height % 128 == 0 else height
    tiles = span // width
    inputs = (hessian_old, gate_rows, up_rows, gate_columns, up_columns)
    vmem = pl.BlockSpec(memory_space=pltpu.VMEM)
    hbm = pl.BlockSpec(memory_space=pltpu.HBM)
    gathered = pl.pallas_call(
        functools.partial(gather_kernel, (n_row, n_z, n_y, n_k, tiles, width)),
        out_shape=(
            pltpu.VMEM((height, span), jnp.float32),
            pltpu.VMEM((n_col, piece, height), jnp.bfloat16),
            pltpu.VMEM((n_row, tiles, depth, width), jnp.bfloat16),
        ),
        in_specs=[hbm] * len(inputs),
        out_specs=(vmem, vmem, vmem),
        scratch_shapes=[
            pltpu.VMEM((piece, height), jnp.bfloat16),
            pltpu.VMEM((piece, height), jnp.bfloat16),
            pltpu.VMEM((tiles, depth, width), jnp.bfloat16),
            pltpu.VMEM((tiles, depth, width), jnp.bfloat16),
            pltpu.SemaphoreType.DMA((2 + 2 * tiles,)),
            pltpu.SemaphoreType.DMA,
            pltpu.SemaphoreType.DMA((max(n_z - 1, 1),)),
            pltpu.SemaphoreType.DMA((n_z,)),
            pltpu.SemaphoreType.DMA((n_z * n_y,)),
            pltpu.SemaphoreType.DMA((max(n_row - 1, 1), tiles)),
            pltpu.SemaphoreType.DMA((n_col,)),
            pltpu.SemaphoreType.DMA((n_row, tiles)),
        ],
        compiler_params=pltpu.CompilerParams(collective_id=0, has_side_effects=True, vmem_limit_bytes=24 * 1024 * 1024),
        name="gather",
    )(*(pltpu.with_memory_space_constraint(a, pltpu.HBM) for a in inputs))
    return pl.pallas_call(
        functools.partial(product_kernel, block),
        out_shape=jax.ShapeDtypeStruct((height, span), jnp.float32),
        in_specs=[vmem] * 3,
        out_specs=hbm,
        scratch_shapes=[pltpu.VMEM((height, span), jnp.float32), pltpu.SemaphoreType.DMA((height // block,))],
        compiler_params=pltpu.CompilerParams(vmem_limit_bytes=24 * 1024 * 1024),
        name="product",
    )(*gathered)


def solution(mesh):
    in_specs = (P("row", "col"), P("col", "row"), P("col", "row"), P("row", "col"), P("row", "col"))
    out_specs = P("row", "col")
    step = functools.partial(body, mesh.shape["row"], mesh.shape["col"])
    return jax.shard_map(step, mesh=mesh, in_specs=in_specs, out_specs=out_specs, check_vma=False)
```

```python
import functools

import jax
import jax.numpy as jnp
from jax import lax
from jax.experimental import pallas as pl
from jax.experimental.pallas import tpu as pltpu
from jax.sharding import PartitionSpec as P

MESH = pl.DeviceIdType.MESH


def silu_product(gate, up):
    return (jax.nn.silu(gate.astype(jnp.float32)) * up.astype(jnp.float32)).astype(jnp.bfloat16)


def partner(z, d, size):
    if size & (size - 1):
        return lax.rem(z + d, size), lax.rem(z + size - d, size)
    out, bit = z, 1
    while bit < size:
        if d & bit:
            out = out + bit * (1 - 2 * lax.rem(z // bit, 2))
        bit *= 2
    return out, out


def gather_kernel(dims, old_hbm, gr_hbm, ur_hbm, gc_hbm, uc_hbm, old, rows, cols, gr, ur, gc, uc, in_sem, old_sem, z_sem, y_sem, k_sem, x_sem, row_recv, col_recv):
    n_row, n_z, n_y, n_k, tiles, width, splits, cuts = dims
    n_col = n_z * n_y * n_k
    r = lax.axis_index("row")
    c = lax.axis_index("col")
    k = lax.rem(c, n_k)
    y = lax.rem(c // n_k, n_y)
    z = c // (n_k * n_y)

    def at(z_, y_, k_):
        return (z_ * n_y + y_) * n_k + k_

    z_to = [partner(z, d, n_z)[0] for d in range(1, n_z)]
    z_from = [partner(z, d, n_z)[1] for d in range(1, n_z)]
    other_y = [lax.rem(y + 1, n_y)] if n_y > 1 else []
    other_k = [lax.rem(k + 1, n_k)] if n_k > 1 else []
    r_to = [lax.rem(r + d, n_row) for d in range(1, n_row)]
    r_from = [lax.rem(r + n_row - d, n_row) for d in range(1, n_row)]

    barrier = pltpu.get_barrier_semaphore()
    peers = [{"col": at(t, y, k)} for t in z_to] + [{"col": at(z, t, k)} for t in other_y] + [{"col": at(z, y, t)} for t in other_k]
    peers += [{"row": t} for t in r_to]
    for peer in peers:
        pl.semaphore_signal(barrier, inc=1, device_id=peer, device_id_type=MESH)

    thick = gr.shape[0] // splits
    deep = gc.shape[1] // cuts
    chunks = [(j, pl.ds(q * deep, deep), j * cuts + q) for j in range(tiles) for q in range(cuts)]
    row_loads = [pltpu.make_async_copy(gr_hbm, gr, in_sem.at[0]), pltpu.make_async_copy(ur_hbm, ur, in_sem.at[1])]
    col_loads = []
    for j, part, n in chunks:
        across = pl.ds(j * width, width)
        col_loads.append((
            pltpu.make_async_copy(gc_hbm.at[part, across], gc.at[j, part], in_sem.at[2 + 2 * n]),
            pltpu.make_async_copy(uc_hbm.at[part, across], uc.at[j, part], in_sem.at[3 + 2 * n])))
    for load in row_loads:
        load.start()
    for pair in col_loads:
        for load in pair:
            load.start()
    old_load = pltpu.make_async_copy(old_hbm, old, old_sem)

    started = []

    def row_copy(piece, h, sem, device):
        part = rows.at[piece, pl.ds(h * thick, thick)]
        return pltpu.make_async_remote_copy(
            src_ref=part, dst_ref=part, send_sem=sem, recv_sem=row_recv.at[piece, h],
            device_id={"col": device}, device_id_type=MESH)

    def send_row(piece, h, sem, device):
        copy = row_copy(piece, h, sem, device)
        copy.start()
        started.append(copy)

    def wait_row(piece, h):
        row_copy(piece, h, k_sem.at[0, 0], c).wait_recv()

    def col_copy(s, chunk, sem, device):
        j, part, n = chunk
        part = cols.at[j, s, part]
        return pltpu.make_async_remote_copy(
            src_ref=part, dst_ref=part, send_sem=sem, recv_sem=col_recv.at[s, n],
            device_id={"row": device}, device_id_type=MESH)

    def form_cols(chunk):
        j, part, n = chunk
        for load in col_loads[n]:
            load.wait()
        cols[j, r, part] = silu_product(gc[j, part], uc[j, part])

    def send_cols(chunk):
        for i, t in enumerate(r_to):
            copy = col_copy(r, chunk, x_sem.at[i, chunk[2]], t)
            copy.start()
            started.append(copy)

    def send_own_rows():
        for h in range(splits):
            for t in other_y:
                send_row(c, h, y_sem.at[0, h], at(z, t, k))
            for t in other_k:
                send_row(c, h, k_sem.at[0, h], at(z, y, t))
        for i, t in enumerate(z_to):
            for h in range(splits):
                send_row(c, h, z_sem.at[i, h], at(t, y, k))

    for load in row_loads:
        load.wait()
    rows[c] = silu_product(gr[...], ur[...])
    pl.semaphore_wait(barrier, len(peers))
    send_own_rows()
    form_cols(chunks[0])
    send_cols(chunks[0])
    for chunk in chunks[1:]:
        form_cols(chunk)
        send_cols(chunk)
    old_load.start()

    used = 1
    for t in other_y:
        for h in range(splits):
            wait_row(at(z, t, k), h)
            for u in other_k:
                send_row(at(z, t, k), h, k_sem.at[used, h], at(z, y, u))
    used += len(other_y)
    for i, s in enumerate(z_from):
        for h in range(splits):
            wait_row(at(s, y, k), h)
            for t in other_y:
                send_row(at(s, y, k), h, y_sem.at[1 + i, h], at(z, t, k))
            for u in other_k:
                send_row(at(s, y, k), h, k_sem.at[used + i, h], at(z, y, u))
    used += len(z_from)
    for i, s in enumerate(z_from):
        for t in other_y:
            for h in range(splits):
                wait_row(at(s, t, k), h)
                for u in other_k:
                    send_row(at(s, t, k), h, k_sem.at[used + i, h], at(z, y, u))
    for t in other_k:
        for s in [z] + z_from:
            for u in [y] + other_y:
                for h in range(splits):
                    wait_row(at(s, u, t), h)
    for s in r_from:
        for chunk in chunks:
            col_copy(s, chunk, x_sem.at[0, 0], r).wait_recv()
    old_load.wait()

    for copy in started:
        copy.wait_send()


def product_kernel(block, old, rows, cols, out_hbm, out, sem):
    n_col, piece, height = rows.shape
    tiles, n_row, depth, width = cols.shape
    tokens = n_col * piece
    stores = []
    for m in range(height // block):
        here = pl.ds(m * block, block)
        left = rows[:, :, here].reshape(tokens, block)
        for j in range(tiles):
            there = pl.ds(j * width, width)
            right = cols[j].reshape(tokens, width)
            total = lax.dot_general(left, right, (((0,), (0,)), ((), ())), preferred_element_type=jnp.float32)
            total = total * (1.0 / tokens) if tokens & (tokens - 1) == 0 else total / tokens
            out[here, there] = 0.5 * old[here, there] + total
        store = pltpu.make_async_copy(out.at[here], out_hbm.at[here], sem.at[m])
        store.start()
        stores.append(store)
    for store in stores:
        store.wait()


def body(n_row, n_col, hessian_old, gate_rows, up_rows, gate_columns, up_columns):
    n_k = 2 if n_col % 2 == 0 else 1
    n_y = 2 if (n_col // n_k) % 2 == 0 else 1
    n_z = n_col // (n_k * n_y)
    height, span = hessian_old.shape
    piece = gate_rows.shape[0]
    depth = gate_columns.shape[0]
    width = 256 if span % 256 == 0 else span
    block = 128 if height % 128 == 0 else height
    tiles = span // width
    splits = 2 if piece % (16 * 2) == 0 else 1
    cuts = 1 if depth % (16 * 1) == 0 else 1
    inputs = (hessian_old, gate_rows, up_rows, gate_columns, up_columns)
    vmem = pl.BlockSpec(memory_space=pltpu.VMEM)
    hbm = pl.BlockSpec(memory_space=pltpu.HBM)
    gathered = pl.pallas_call(
        functools.partial(gather_kernel, (n_row, n_z, n_y, n_k, tiles, width, splits, cuts)),
        out_shape=(
            pltpu.VMEM((height, span), jnp.float32),
            pltpu.VMEM((n_col, piece, height), jnp.bfloat16),
            pltpu.VMEM((tiles, n_row, depth, width), jnp.bfloat16),
        ),
        in_specs=[hbm] * len(inputs),
        out_specs=(vmem, vmem, vmem),
        scratch_shapes=[
            pltpu.VMEM((piece, height), jnp.bfloat16),
            pltpu.VMEM((piece, height), jnp.bfloat16),
            pltpu.VMEM((tiles, depth, width), jnp.bfloat16),
            pltpu.VMEM((tiles, depth, width), jnp.bfloat16),
            pltpu.SemaphoreType.DMA((2 + 2 * tiles * cuts,)),
            pltpu.SemaphoreType.DMA,
            pltpu.SemaphoreType.DMA((max(n_z - 1, 1), splits)),
            pltpu.SemaphoreType.DMA((n_z, splits)),
            pltpu.SemaphoreType.DMA((n_z * n_y, splits)),
            pltpu.SemaphoreType.DMA((max(n_row - 1, 1), tiles * cuts)),
            pltpu.SemaphoreType.DMA((n_col, splits)),
            pltpu.SemaphoreType.DMA((n_row, tiles * cuts)),
        ],
        compiler_params=pltpu.CompilerParams(collective_id=0, has_side_effects=True, vmem_limit_bytes=24 * 1024 * 1024),
        name="gather",
    )(*(pltpu.with_memory_space_constraint(a, pltpu.HBM) for a in inputs))
    return pl.pallas_call(
        functools.partial(product_kernel, block),
        out_shape=jax.ShapeDtypeStruct((height, span), jnp.float32),
        in_specs=[vmem] * 3,
        out_specs=hbm,
        scratch_shapes=[pltpu.VMEM((height, span), jnp.float32), pltpu.SemaphoreType.DMA((height // block,))],
        compiler_params=pltpu.CompilerParams(vmem_limit_bytes=24 * 1024 * 1024),
        name="product",
    )(*gathered)


def solution(mesh):
    in_specs = (P("row", "col"), P("col", "row"), P("col", "row"), P("row", "col"), P("row", "col"))
    out_specs = P("row", "col")
    step = functools.partial(body, mesh.shape["row"], mesh.shape["col"])
    return jax.shard_map(step, mesh=mesh, in_specs=in_specs, out_specs=out_specs, check_vma=False)
```
